256 devices in a mesh: seq: 64 (over x, z, core), head: 4 (over y).
Axes of the slice: x: 4, y: 4, z: 8, core: 2. Of those that a mesh axis runs over, the one named last changes fastest.
Arguments:
- tree_queries: bfloat16 [4, 64, 128, 128], P(None, 'seq', 'head'), may hold values from -100 to 100
- tree_keys: bfloat16 [4, 64, 8, 128], P(None, 'seq', 'head'), may hold values from -12 to 12
- tree_values: bfloat16 [4, 64, 8, 128], P(None, 'seq', 'head'), may hold values from -6 to 6
- cache_keys: bfloat16 [4, 40960, 8, 128], P(None, 'seq', 'head'), may hold values from -6 to 6
- cache_values: bfloat16 [4, 40960, 8, 128], P(None, 'seq', 'head'), may hold values from -6 to 6
- out_weight: bfloat16 [16384, 16384], P('head', 'seq'), may hold values from -0.8984375 to 0.8984375
- context_lengths: int32 [4], replicated, may hold values from 5120 to 40952, as said below
- parents: int32 [4, 64], replicated, may hold values from -1 to 62, as said below
- accepted_nodes: int32 [4, 8], replicated, may hold values from 0 to 63, as said below
- accepted_count: int32 [4], replicated, may hold values from 1 to 8
Outputs:
- projected: bfloat16 [256, 16384], P('head', 'seq')
- keys_out: bfloat16 [4, 40960, 8, 128], P(None, 'seq', 'head')
- values_out: bfloat16 [4, 40960, 8, 128], P(None, 'seq', 'head')
The draws below stay inside these ranges and needn't reach their ends.
Inputs may be any that keep to these rules, and one draw needn't show every extreme that they name: Request r's cache holds positions 0 to context_lengths[r] - 1; some request has the largest value in every draw. parents[r, 0] = -1 marks the root; for i >= 1, 0 <= parents[r, i] < i. `accepted_nodes`: each row lists distinct tree nodes in increasing order, the first being the root 0; entries j >= accepted_count[r] are not used.
All inputs are finite; a program needn't handle non-finite values.
Results may differ from the reference program's by a relative error of at most 0.0051.
Values may be sent and summed in bfloat16 or wider, within the bound.
No kernel may reach another device: no remote copies, remote signals or barrier semaphores. Data moves between devices by JAX's collectives and lax.ppermute only.
A program may use at most 64 MiB of HBM per device.

```python
import math
import jax
import jax.numpy as jnp
from jax import lax

D = 16384
HQ = 128
KVH = 8
HD = 128
REQ = 4
NODES = 64
ACC = 8
CTX_DEV = 640
CAP = 40960
N_SEQ = 64


def draw_cache_keys(key, part):
    drawn = jnp.clip(jax.random.normal(jax.random.fold_in(key, 21), (REQ, CAP, KVH, HD), jnp.float32), -6.0, 6.0)
    return drawn.astype(jnp.bfloat16)


def draw_tree_queries(key, part):
    drawn = jnp.clip(2.0 * jax.random.normal(jax.random.fold_in(key, 31), (REQ, NODES, HQ, HD), jnp.float32), -12.0, 12.0)
    return drawn.astype(jnp.bfloat16)


def draw_context_lengths(key, part):
    shortest = CAP // 8
    longest = CAP - ACC
    drawn = jax.random.randint(jax.random.fold_in(key, 41), (REQ,), shortest, longest + 1)
    chosen = jax.random.randint(jax.random.fold_in(key, 42), (), 0, REQ)
    return jnp.where(jnp.arange(REQ) == chosen, longest, drawn).astype(jnp.int32)


def draw_parents(key, part):
    bounds = jnp.maximum(jnp.arange(NODES, dtype=jnp.int32), 1)
    drawn = jax.random.randint(jax.random.fold_in(key, 51), (REQ, NODES), 0, bounds[None, :])
    chosen = jax.random.randint(jax.random.fold_in(key, 52), (), 0, REQ)
    last_column = jnp.where(jnp.arange(REQ) == chosen, NODES - 2, drawn[:, NODES - 1])
    drawn = drawn.at[:, NODES - 1].set(last_column)
    return drawn.at[:, 0].set(-1).astype(jnp.int32)


def draw_accepted_nodes(key, part):
    subkeys = jax.random.split(jax.random.fold_in(key, 61), REQ)
    picks = jax.vmap(lambda single: jax.random.permutation(single, NODES - 1)[:ACC - 1] + 1)(subkeys)
    joined = jnp.sort(jnp.concatenate([jnp.zeros((REQ, 1), jnp.int32), picks.astype(jnp.int32)], axis=1), axis=1)
    chosen = jax.random.randint(jax.random.fold_in(key, 62), (), 0, REQ)
    return joined.at[chosen, ACC - 1].set(NODES - 1).astype(jnp.int32)


def draw_accepted_count(key, part):
    drawn = jax.random.randint(jax.random.fold_in(key, 71), (REQ,), 1, ACC + 1)
    chosen = jax.random.randint(jax.random.fold_in(key, 72), (), 0, REQ)
    return jnp.where(jnp.arange(REQ) == chosen, ACC, drawn).astype(jnp.int32)


def levels(stream_key, extent, cuts, least, top_value):
    gain, own = 1.0, jax.random.fold_in(stream_key, 6)
    for position, parts in cuts:
        steps = jnp.exp(jax.random.uniform(jax.random.fold_in(own, position), (parts,), jnp.float32, least / len(cuts), top_value / len(cuts)))
        gain = gain * jnp.repeat(steps, extent[position] // parts).reshape([-1 if axis == position else 1 for axis in range(len(extent))])
    return gain


def bell_draw(stream_key, dims, scale, reach, shards=(), held_as=jnp.bfloat16):
    values = jax.random.normal(stream_key, dims, jnp.float32) * scale
    if len(shards) > 0:
        values = levels(stream_key, dims, shards, -0.22, 0.18) * values
    return jnp.clip(values, min=-reach, max=reach).astype(held_as)


def setup_inputs(seed: int = 0) -> dict:
    seeds = jax.random.split(jax.random.key(seed), 11)
    return {
        "tree_queries": draw_tree_queries(jax.random.fold_in(seeds[10], 71), 0),
        "tree_keys": bell_draw(seeds[1], (REQ, NODES, KVH, HD), 2.0, 12.0, ((1, 64), (2, 4))),
        "tree_values": bell_draw(seeds[2], (REQ, NODES, KVH, HD), 1.0, 6.0, ((1, 64), (2, 4))),
        "cache_keys": draw_cache_keys(jax.random.fold_in(seeds[10], 71), 0),
        "cache_values": bell_draw(seeds[4], (REQ, CAP, KVH, HD), 1.0, 6.0, ((1, 64), (2, 4))),
        "out_weight": bell_draw(seeds[5], (HQ * HD, D), 0.15, 0.8984375, ((0, 4), (1, 64))),
        "context_lengths": draw_context_lengths(jax.random.fold_in(seeds[10], 71), 0),
        "parents": draw_parents(jax.random.fold_in(seeds[10], 71), 0),
        "accepted_nodes": draw_accepted_nodes(jax.random.fold_in(seeds[10], 71), 0),
        "accepted_count": draw_accepted_count(jax.random.fold_in(seeds[10], 71), 0),
    }


NEG = -1e+30

def ancestors(parents):
    count_nodes = parents.shape[1]
    columns = jnp.arange(count_nodes, dtype=jnp.int32)
    linked = (parents[:, :, None] == columns[None, None, :]) | (columns[:, None] == columns[None, :])[None]
    closure = linked.astype(jnp.float32)
    for rounds in range(max(count_nodes - 1, 1).bit_length()):
        closure = jnp.minimum(jnp.matmul(closure, closure, precision=lax.Precision.HIGHEST), 1.0)
    return closure

def reference(tree_queries, tree_keys, tree_values, cache_keys, cache_values, out_weight, context_lengths, parents, accepted_nodes, accepted_count):
    scale_factor = 1.0 / math.sqrt(HD)
    group_size = HQ // KVH
    closure = ancestors(parents)
    outputs = []
    for request in range(REQ):
        grouped = tree_queries[request].astype(jnp.float32).reshape(NODES, KVH, group_size, HD)
        cache_k = cache_keys[request].astype(jnp.float32).reshape(N_SEQ, CTX_DEV, KVH, HD)
        cache_v = cache_values[request].astype(jnp.float32).reshape(N_SEQ, CTX_DEV, KVH, HD)
        tree_k = tree_keys[request].astype(jnp.float32)
        tree_v = tree_values[request].astype(jnp.float32)
        in_cache = (jnp.arange(CAP, dtype=jnp.int32) < context_lengths[request]).reshape(N_SEQ, CTX_DEV)
        tree_allowed = closure[request] > 0.5

        def per_head(operands):
            queries, keys_c, values_c, keys_t, values_t = operands
            scores_c = jnp.einsum('ngd,bpd->ngbp', queries, keys_c) * scale_factor
            mask_c = in_cache[None, None, :, :]
            top_c = lax.optimization_barrier(jnp.max(jnp.where(mask_c, scores_c, NEG), axis=-1))
            weights_c = jnp.where(mask_c, jnp.exp(scores_c - top_c[..., None]), 0.0)
            scores_t = jnp.einsum('ngd,pd->ngp', queries, keys_t) * scale_factor
            mask_t = tree_allowed[:, None, :]
            top_t = lax.optimization_barrier(jnp.max(jnp.where(mask_t, scores_t, NEG), axis=-1))
            weights_t = jnp.where(mask_t, jnp.exp(scores_t - top_t[..., None]), 0.0)
            row_top = jnp.maximum(lax.optimization_barrier(jnp.max(top_c, axis=-1)), top_t)
            factor_c = jnp.exp(top_c - row_top[..., None])
            factor_t = jnp.exp(top_t - row_top)
            row_sum = lax.optimization_barrier(jnp.sum(lax.optimization_barrier(jnp.sum(weights_c, axis=-1)) * factor_c, axis=-1)) + lax.optimization_barrier(jnp.sum(weights_t, axis=-1)) * factor_t
            rounded_c = lax.optimization_barrier(weights_c.astype(jnp.bfloat16)).astype(jnp.float32)
            rounded_t = lax.optimization_barrier(weights_t.astype(jnp.bfloat16)).astype(jnp.float32)
            block_num = jnp.einsum('ngbp,bpd->ngbd', rounded_c, values_c)
            numerator = lax.optimization_barrier(jnp.sum(block_num * factor_c[..., None], axis=2))
            numerator = numerator + jnp.einsum('ngp,pd->ngd', rounded_t, values_t) * factor_t[..., None]
            return (numerator / row_sum[:, :, None]).astype(jnp.bfloat16)
        per_head_out = lax.map(per_head, (jnp.moveaxis(grouped, 1, 0), jnp.moveaxis(cache_k, 2, 0), jnp.moveaxis(cache_v, 2, 0), jnp.moveaxis(tree_k, 1, 0), jnp.moveaxis(tree_v, 1, 0)))
        outputs.append(jnp.moveaxis(per_head_out, 0, 1).reshape(NODES, HQ * HD))
    attention = jnp.concatenate(outputs, axis=0)
    projected = jnp.dot(attention, out_weight, preferred_element_type=jnp.float32).astype(jnp.bfloat16)
    rows_index = jnp.arange(REQ, dtype=jnp.int32)[:, None]
    steps_index = jnp.arange(ACC, dtype=jnp.int32)[None, :]
    targets = jnp.where(steps_index < accepted_count[:, None], context_lengths[:, None] + steps_index, CAP).astype(jnp.int32)
    keys_out = cache_keys.at[rows_index, targets].set(tree_keys[rows_index, accepted_nodes], mode='drop')
    values_out = cache_values.at[rows_index, targets].set(tree_values[rows_index, accepted_nodes], mode='drop')
    return (projected, keys_out, values_out)
```

```python
import functools
import math

import jax
import jax.numpy as jnp
from jax import lax
from jax.experimental import pallas as pl
from jax.experimental.pallas import tpu as pltpu
from jax.sharding import Mesh
from jax.sharding import PartitionSpec as P

NEG = -1e30
BF16 = jnp.bfloat16
F32 = jnp.float32
CHIPS = ("x", "z")
STAT_ROWS = 8


def iota(shape, dim):
    return lax.broadcasted_iota(jnp.int32, shape, dim)


def split_heads_kernel(core_ref, k_ref, v_ref, keep_k, send_k, keep_v, send_v, copy_k, copy_v, wide_k, wide_v):
    core = core_ref[0]
    rows = keep_k.shape[1]
    for source, keep, send, copy, wide in (
        (k_ref, keep_k, send_k, copy_k, wide_k),
        (v_ref, keep_v, send_v, copy_v, wide_v),
    ):
        block = source[0]
        copy[0] = block
        wide[...] = block.astype(F32)
        first = wide[pl.ds(0, rows, stride=2), :].astype(BF16)
        second = wide[pl.ds(1, rows, stride=2), :].astype(BF16)

        @pl.when(core == 0)
        def _(keep=keep, send=send, first=first, second=second):
            keep[0] = first
            send[0] = second

        @pl.when(core != 0)
        def _(keep=keep, send=send, first=first, second=second):
            keep[0] = second
            send[0] = first


def split_heads(core, keys, values):
    requests, both, width = keys.shape
    rows = both // 2
    half = jax.ShapeDtypeStruct((requests, rows, width), BF16)
    full = jax.ShapeDtypeStruct((requests, both, width), BF16)
    half_spec = pl.BlockSpec((1, rows, width), lambda r, *_: (r, 0, 0))
    full_spec = pl.BlockSpec((1, both, width), lambda r, *_: (r, 0, 0))
    return pl.pallas_call(
        split_heads_kernel,
        grid_spec=pltpu.PrefetchScalarGridSpec(
            num_scalar_prefetch=1,
            grid=(requests,),
            in_specs=[full_spec, full_spec],
            out_specs=[half_spec] * 4 + [full_spec] * 2,
            scratch_shapes=[pltpu.VMEM((both, width), F32)] * 2,
        ),
        out_shape=[half] * 4 + [full] * 2,
        name="split_heads",
    )(core, keys, values)


def three_parts(exact):
    high = exact.astype(BF16)
    rest = exact - high.astype(F32)
    middle = rest.astype(BF16)
    return high, middle, (rest - middle.astype(F32)).astype(BF16)


def attend_kernel(scale, info_ref, q_ref, ka_ref, kb_ref, va_ref, vb_ref, out_ref, wide_v):
    request = pl.program_id(0)
    keys, width = ka_ref.shape[1], ka_ref.shape[2]
    sources, rows = q_ref.shape[0], q_ref.shape[1]
    count = sources * rows
    pieces = out_ref.shape[0]
    piece_rows = count // pieces

    @pl.when(pl.program_id(1) == 0)
    def _():
        wide_v[0:keys, 0:width] = va_ref[0]
        wide_v[keys : 2 * keys, 0:width] = vb_ref[0]
        wide_v[:, width : 2 * width] = jnp.ones((2 * keys, width), BF16)

    left = info_ref[request] - info_ref[4]
    right = info_ref[request] - info_ref[5]

    def run(masked):
        queries = q_ref[...].reshape(count, width)
        contract = (((1,), (1,)), ((), ()))
        first = lax.dot_general(queries, ka_ref[0], contract, preferred_element_type=F32)
        second = lax.dot_general(queries, kb_ref[0], contract, preferred_element_type=F32)
        if masked:
            position = iota((1, keys), 1)
            first = first + jnp.where(position < left, 0.0, NEG)
            second = second + jnp.where(position < right, 0.0, NEG)
        top = jnp.maximum(jnp.max(first, axis=1, keepdims=True), jnp.max(second, axis=1, keepdims=True))
        factor = scale * math.log2(math.e)
        weight_a = jnp.exp2((first - top) * factor).astype(BF16)
        weight_b = jnp.exp2((second - top) * factor).astype(BF16)
        total = jnp.dot(weight_a, wide_v[0:keys, :], preferred_element_type=F32) + jnp.dot(
            weight_b, wide_v[keys : 2 * keys, :], preferred_element_type=F32
        )
        row_sum = total[:, width:]
        mean = (total[:, :width] / row_sum).astype(BF16)
        level = top * scale + jnp.log(row_sum)
        for piece in range(pieces):
            part = slice(piece * piece_rows, (piece + 1) * piece_rows)
            out_ref[piece, 0:piece_rows, :] = mean[part]
            square = (piece_rows, width)
            line = jnp.sum(jnp.where(iota(square, 0) == iota(square, 1), level[part], 0.0), axis=0, keepdims=True)
            high, middle, low = (item.astype(F32) for item in three_parts(line))
            index = iota((STAT_ROWS, width), 0)
            stats = jnp.where(index == 0, high, jnp.where(index == 1, middle, jnp.where(index == 2, low, 0.0)))
            out_ref[piece, piece_rows : piece_rows + STAT_ROWS, :] = stats.astype(BF16)

    whole = jnp.logical_and(left >= keys, right >= keys)

    @pl.when(whole)
    def _():
        run(False)

    @pl.when(jnp.logical_not(whole))
    def _():
        run(True)


def attend(info, gathered, ka, kb, va, vb, scale, tiles=4):
    requests, keys, width = ka.shape
    sources = gathered.shape[0]
    rows = 32
    piece_rows = 128
    pieces = sources * rows // piece_rows
    per_tile = pieces // tiles
    cache = pl.BlockSpec((1, keys, width), lambda r, t, *_: (r, 0, 0))
    return pl.pallas_call(
        functools.partial(attend_kernel, scale),
        grid_spec=pltpu.PrefetchScalarGridSpec(
            num_scalar_prefetch=1,
            grid=(requests, tiles),
            in_specs=[pl.BlockSpec((sources // tiles, rows, width), lambda r, t, *_: (t, r, 0))] + [cache] * 4,
            out_specs=pl.BlockSpec((per_tile, piece_rows + STAT_ROWS, width), lambda r, t, *_: (r * tiles + t, 0, 0)),
            scratch_shapes=[pltpu.VMEM((2 * keys, 2 * width), BF16)],
        ),
        out_shape=jax.ShapeDtypeStruct((requests * pieces, piece_rows + STAT_ROWS, width), BF16),
        name="attend",
    )(info, gathered, ka, kb, va, vb)


def tree_kernel(scale, where_ref, q_ref, tree_ref, parent_ref, mean_ref, level_ref):
    request, slot = where_ref[0], where_ref[1]
    chips, width = tree_ref.shape[0], tree_ref.shape[2]
    nodes = parent_ref.shape[0]
    square = (nodes, nodes)
    linked = jnp.logical_or(parent_ref[...] == iota(square, 1), iota(square, 0) == iota(square, 1))
    closure = linked.astype(F32)
    for _ in range(max(nodes - 1, 1).bit_length()):
        narrow = closure.astype(BF16)
        closure = jnp.minimum(jnp.dot(narrow, narrow, preferred_element_type=F32), 1.0)
    queries = q_ref[...].reshape(-1, width)
    count = queries.shape[0]
    heads = 16
    of_row = (iota((count, nodes), 0) // heads + slot * (count // heads) == iota((count, nodes), 1)).astype(BF16)
    mine = jnp.dot(of_row, closure.astype(BF16), preferred_element_type=F32).astype(BF16)
    tree = tree_ref[...]
    keys = tree[:, 0:8, :].reshape(chips * 8, width)
    values = tree[:, 8:16, :].reshape(chips * 8, width)
    column = iota((nodes, chips * 8), 1)
    node = (column // 8) * 2 + column % 2
    spread = jnp.logical_and(node == iota((nodes, chips * 8), 0), (column // 2) % 4 == request).astype(BF16)
    allowed = jnp.dot(mine, spread, preferred_element_type=F32) > 0.5
    scores = lax.dot_general(queries, keys, (((1,), (1,)), ((), ())), preferred_element_type=F32) * scale
    top = jnp.max(jnp.where(allowed, scores, NEG), axis=1, keepdims=True)
    weight = jnp.where(allowed, jnp.exp(scores - top), 0.0)
    row_sum = jnp.sum(weight, axis=1, keepdims=True)
    total = jnp.dot(weight.astype(BF16), values, preferred_element_type=F32)
    mean_ref[...] = total / row_sum
    level_ref[...] = jnp.broadcast_to(top + jnp.log(row_sum), (count, width))


def tree_part(where, gathered, parent, scale):
    sources, _, width = gathered.shape
    flat = jax.ShapeDtypeStruct((128, width), F32)
    return pl.pallas_call(
        functools.partial(tree_kernel, scale),
        grid_spec=pltpu.PrefetchScalarGridSpec(
            num_scalar_prefetch=1,
            grid=(1,),
            in_specs=[
                pl.BlockSpec((4, 32, width), lambda i, w: (w[1], w[0], 0)),
                pl.BlockSpec((sources, 16, width), lambda i, w: (0, 8, 0)),
                pl.BlockSpec(parent.shape, lambda i, w: (0, 0)),
            ],
            out_specs=[pl.BlockSpec((128, width), lambda i, w: (0, 0))] * 2,
        ),
        out_shape=[flat, flat],
        name="tree_part",
    )(where, gathered, gathered, parent)


def merge_kernel(parts_ref, mean_ref, level_ref, out_ref):
    sources, width = parts_ref.shape[0], parts_ref.shape[2]
    rows = mean_ref.shape[0]
    stats = parts_ref[:, rows : rows + STAT_ROWS, :].astype(F32)
    lines = stats[:, 0, :] + stats[:, 1, :] + stats[:, 2, :]
    lines = jnp.concatenate([lines, jnp.full((width - sources, rows), NEG, F32)], axis=0)
    levels = jnp.transpose(lines)
    tree_level = level_ref[...]
    top = jnp.maximum(jnp.max(levels, axis=1, keepdims=True), tree_level[:, 0:1])
    scales = jnp.exp(levels - top)
    tree_scale = jnp.exp(tree_level - top)
    row_sum = jnp.sum(scales, axis=1, keepdims=True) + tree_scale
    total = mean_ref[...] * tree_scale
    for source in range(sources):
        total = total + parts_ref[source, 0:rows, :].astype(F32) * scales[:, source : source + 1]
    merged = (total / row_sum).astype(BF16)
    heads, nodes = 16, rows // 16
    square = (rows, rows)
    wanted = (iota(square, 0) % nodes) * heads + iota(square, 0) // nodes
    order = (wanted == iota(square, 1)).astype(BF16)
    ordered = jnp.dot(order, merged, preferred_element_type=F32)
    line = jnp.concatenate([ordered[h * nodes : (h + 1) * nodes, :] for h in range(heads)], axis=1).astype(BF16)
    for target in range(out_ref.shape[0]):
        out_ref[target] = line


def merge(parts, mean, level):
    sources, _, width = parts.shape
    rows = mean.shape[0]
    return pl.pallas_call(
        merge_kernel,
        out_shape=jax.ShapeDtypeStruct((sources, rows // 16, 16 * width), BF16),
        name="merge",
    )(parts, mean, level)


def project_kernel(core_ref, mine_ref, other_ref, weight_ref, out_ref):
    core = core_ref[0]
    half = mine_ref.shape[1]
    first = weight_ref[pl.ds(pl.multiple_of(core * half, half), half), :]
    second = weight_ref[pl.ds(pl.multiple_of((1 - core) * half, half), half), :]
    out_ref[...] = jnp.dot(mine_ref[...], first, preferred_element_type=F32) + jnp.dot(
        other_ref[...], second, preferred_element_type=F32
    )


def project(core, mine, other, weight):
    return pl.pallas_call(
        project_kernel,
        in_specs=[pl.BlockSpec(memory_space=pltpu.SMEM)] + [pl.BlockSpec(memory_space=pltpu.VMEM)] * 3,
        out_shape=jax.ShapeDtypeStruct((mine.shape[0], weight.shape[1]), F32),
        name="project",
    )(core, mine, other, weight)


def append_kernel(info_ref, rows_k, rows_v, keys_in, values_in, keys_out, values_out, sem_k, sem_v):
    local = keys_out.shape[1]
    requests, most = info_ref.shape[0], rows_k.shape[0] // keys_out.shape[0]
    for request in range(requests):
        start, count = info_ref[request, 0], info_ref[request, 1]

        def place(j, carry, request=request, start=start, count=count):
            target = start + j

            @pl.when(jnp.logical_and(j < count, jnp.logical_and(target >= 0, target < local)))
            def _():
                copy_k = pltpu.make_async_copy(rows_k.at[request * most + j], keys_out.at[request, target], sem_k)
                copy_v = pltpu.make_async_copy(rows_v.at[request * most + j], values_out.at[request, target], sem_v)
                copy_k.start()
                copy_v.start()
                copy_k.wait()
                copy_v.wait()

            return carry

        lax.fori_loop(0, most, place, 0)


def append(info, rows_k, rows_v, keys, values):
    anywhere = pl.BlockSpec(memory_space=pl.ANY)
    return pl.pallas_call(
        append_kernel,
        in_specs=[pl.BlockSpec(memory_space=pltpu.SMEM)]
        + [pl.BlockSpec(memory_space=pltpu.VMEM)] * 2
        + [anywhere] * 2,
        out_specs=[anywhere] * 2,
        out_shape=[jax.ShapeDtypeStruct(keys.shape, BF16)] * 2,
        input_output_aliases={3: 0, 4: 1},
        scratch_shapes=[pltpu.SemaphoreType.DMA, pltpu.SemaphoreType.DMA],
        name="append",
    )(info, rows_k, rows_v, keys, values)


def swap(block):
    return lax.ppermute(block, "c", [(0, 1), (1, 0)])


def exchange(block, axis):
    return lax.all_to_all(block, axis, 0, 0, tiled=True)


def on_device(queries, tree_k, tree_v, cache_k, cache_v, weight, lengths, parents, accepted, accepted_count):
    requests, local, kv_local, width = cache_k.shape
    heads = queries.shape[2] // kv_local
    chips = lax.axis_size("x") * lax.axis_size("z")
    scale = 1.0 / math.sqrt(width)
    core = lax.axis_index("c")
    x, z = lax.axis_index("x"), lax.axis_index("z")
    chip = x * lax.axis_size("z") + z
    index = chip * 2 + core
    core_vector = core.astype(jnp.int32)[None]
    low = core == 0

    by_head = jnp.concatenate(
        [
            queries.reshape(requests, kv_local, heads, width).transpose(1, 0, 2, 3).reshape(kv_local, -1, width),
            tree_k.reshape(requests, kv_local, width).transpose(1, 0, 2),
            tree_v.reshape(requests, kv_local, width).transpose(1, 0, 2),
        ],
        axis=1,
    )
    own = jnp.where(low, by_head[0], by_head[1])
    other = swap(jnp.where(low, by_head[1], by_head[0]))
    first, second = jnp.where(low, own, other), jnp.where(low, other, own)
    split = requests * heads
    node_q = jnp.stack([first[:split].reshape(requests, heads, width), second[:split].reshape(requests, heads, width)], 1)
    node_t = jnp.stack([first[split:], second[split:]], 1)
    payload = jnp.concatenate([node_q.reshape(-1, width), node_t.reshape(-1, width)], axis=0)
    gathered = exchange(jnp.broadcast_to(payload[None], (chips,) + payload.shape).reshape(-1, width), CHIPS)
    gathered = gathered.reshape(chips, -1, width)

    keep_k, send_k, keep_v, send_v, copy_k, copy_v = split_heads(
        core_vector, cache_k.reshape(requests, -1, width), cache_v.reshape(requests, -1, width)
    )
    other_k, other_v = swap(send_k), swap(send_v)
    offsets = jnp.stack([index * local, (chip * 2 + 1 - core) * local]).astype(jnp.int32)
    info = jnp.concatenate([lengths.astype(jnp.int32), offsets])
    parts = attend(info, gathered, keep_k, other_k, keep_v, other_v, scale)
    parts = exchange(parts.reshape(-1, width), CHIPS).reshape(parts.shape)

    place = jnp.stack([x, z]).astype(jnp.int32)
    parent = lax.dynamic_index_in_dim(parents, x, 0, keepdims=False)[:, None]
    tree_mean, tree_level = tree_part(place, gathered, parent, scale)
    spread = merge(parts, tree_mean, tree_level)
    attention = exchange(spread.reshape(-1, spread.shape[2]), CHIPS)
    partial = project(core_vector, attention, swap(attention), weight)
    shares = exchange(partial, "y").reshape(lax.axis_size("y"), -1, partial.shape[1])
    projected = jnp.sum(shares, axis=0).astype(BF16)

    tree_all = gathered[:, split * 2 :, :].reshape(chips, 2, requests, 2, width)
    tree_all = tree_all.transpose(1, 2, 0, 3, 4).reshape(2, requests, chips * 2, width)
    choose = (accepted[:, :, None] == jnp.arange(chips * 2, dtype=jnp.int32)).astype(BF16)
    picked = jnp.einsum("rjn,krne->krje", choose, tree_all, preferred_element_type=F32).astype(BF16)
    picked_other = swap(picked)
    rows = jnp.stack([jnp.where(low, picked, picked_other), jnp.where(low, picked_other, picked)], axis=3)
    rows = rows.reshape(2, -1, 2, width)
    target = jnp.stack([lengths - index * local, accepted_count], axis=1).astype(jnp.int32)
    keys_out, values_out = append(target, rows[0], rows[1], copy_k.reshape(cache_k.shape), copy_v.reshape(cache_v.shape))
    return projected, keys_out, values_out


def solution(mesh):
    fine = Mesh(mesh.devices.reshape(4, 8, 2, 4), ("x", "z", "c", "y"))
    seq = ("x", "z", "c")
    cache = P(None, seq, "y", None)
    in_specs = (cache, cache, cache, cache, cache, P("y", seq), P(), P(), P(), P())
    out_specs = (P("y", seq), cache, cache)
    return jax.shard_map(on_device, mesh=fine, in_specs=in_specs, out_specs=out_specs, check_vma=False)
```

```python
import functools
import math

import jax
import jax.numpy as jnp
from jax import lax
from jax.experimental import pallas as pl
from jax.experimental.pallas import tpu as pltpu
from jax.sharding import Mesh
from jax.sharding import PartitionSpec as P

NEG = -1e30
BF16 = jnp.bfloat16
F32 = jnp.float32
STAT_ROWS = 8


def iota(shape, dim):
    return lax.broadcasted_iota(jnp.int32, shape, dim)


def split_heads_kernel(where_ref, k_ref, v_ref, copy_k, copy_v, *refs):
    distance, core = pl.program_id(0), where_ref[1]
    outs, wides = refs[:-2], refs[-2:]
    rows = outs[0].shape[0] // 2
    parts = []
    for source, copy, wide in zip((k_ref, v_ref), (copy_k, copy_v), wides):
        copy[...] = source[...]
        wide[...] = source[0].astype(F32)
        parts.append([wide[pl.ds(head, rows, stride=2), :].astype(BF16) for head in range(2)])
    for step in range(len(outs) // 2):
        for mine in range(2):

            @pl.when(jnp.logical_and(distance == step, core == mine))
            def _(step=step, mine=mine):
                for place in range(2):
                    span = slice(place * rows, (place + 1) * rows)
                    outs[2 * step][span, :] = parts[place][mine]
                    outs[2 * step + 1][span, :] = parts[place][1 - mine]


def split_heads(where, keys, values):
    requests, both, width = keys.shape
    full_spec = pl.BlockSpec((1, both, width), lambda d, w: (lax.rem(w[0] + d, requests), 0, 0))
    return pl.pallas_call(
        split_heads_kernel,
        grid_spec=pltpu.PrefetchScalarGridSpec(
            num_scalar_prefetch=1,
            grid=(requests,),
            in_specs=[full_spec, full_spec],
            out_specs=[full_spec] * 2 + [pl.BlockSpec((both, width), lambda d, w: (0, 0))] * (2 * requests),
            scratch_shapes=[pltpu.VMEM((both, width), F32)] * 2,
        ),
        out_shape=[jax.ShapeDtypeStruct(keys.shape, BF16)] * 2
        + [jax.ShapeDtypeStruct((both, width), BF16)] * (2 * requests),
        name="split_heads",
        compiler_params=pltpu.CompilerParams(vmem_limit_bytes=12 << 20),
    )(where, keys, values)


def pack_kernel(q_ref, k_ref, v_ref, out_ref):
    requests = q_ref.shape[0]
    columns, cores = out_ref.shape[1], out_ref.shape[2]
    heads = q_ref.shape[1] // cores
    tree = jnp.concatenate([k_ref[...], v_ref[...]], axis=0)
    for core in range(cores):
        shape = (2 * requests, 2 * requests * cores)
        choose = (iota(shape, 1) == iota(shape, 0) * cores + core).astype(BF16)
        rows = jnp.dot(choose, tree, preferred_element_type=F32).astype(BF16)
        for request in range(requests):
            queries = q_ref[request, core * heads : (core + 1) * heads, :]
            for column in range(columns):
                out_ref[request, column, core, 0:heads, :] = queries
                out_ref[request, column, core, heads:, :] = rows


def pack(queries, tree_k, tree_v, columns, cores):
    requests, heads, width = queries.shape
    rows = heads // cores + 2 * requests
    return pl.pallas_call(
        pack_kernel,
        out_shape=jax.ShapeDtypeStruct((requests, columns, cores, rows, width), BF16),
        name="pack",
        compiler_params=pltpu.CompilerParams(vmem_limit_bytes=4 << 20),
    )(queries, tree_k, tree_v)


def three_parts(exact):
    high = exact.astype(BF16).astype(F32)
    rest = exact - high
    middle = rest.astype(BF16).astype(F32)
    return high, middle, (rest - middle).astype(BF16).astype(F32)


def stat_rows(line):
    high, middle, low = three_parts(line)
    index = iota((STAT_ROWS, line.shape[1]), 0)
    rows = jnp.where(index == 0, high, jnp.where(index == 1, middle, jnp.where(index == 2, low, 0.0)))
    return rows.astype(BF16)


def diagonal(block):
    return jnp.sum(jnp.where(iota(block.shape, 0) == iota(block.shape, 1), block, 0.0), axis=0, keepdims=True)


TILE = 256


def attend_kernel(scale, first, last, entry, info_ref, q_ref, *refs):
    heads, piece_rows = 16, 128
    near_ref, far_ref = refs[:2]
    state_in = () if first else refs[2:4]
    outs = refs[2 if first else 4 : -6]
    k_all, v_all, bias, s0, s1, tops = refs[-6:]
    both, width = near_ref.shape
    keys = both // 2
    nodes_per_tile = TILE // heads
    tiles = q_ref.shape[0] // nodes_per_tile
    factor = scale * math.log2(math.e)
    position = iota((1, keys), 1)
    for part, ref in enumerate((near_ref, far_ref)):
        rows = slice(part * keys, (part + 1) * keys)
        k_all[rows, :] = ref[0:keys, :]
        v_all[rows, 0:width] = ref[keys:both, :]
        bias[:, rows] = jnp.where(position < info_ref[entry + part], 0.0, NEG)
    v_all[:, width : 2 * width] = jnp.ones((both, width), BF16)
    buffers = (s0, s1)

    def score(tile):
        nodes = slice(tile * nodes_per_tile, (tile + 1) * nodes_per_tile)
        queries = q_ref[nodes, 0:heads, :].reshape(TILE, width)
        scores = lax.dot_general(queries, k_all[...], (((1,), (1,)), ((), ())), preferred_element_type=F32)
        scores = scores + bias[...]
        buffers[tile % 2][...] = scores
        tops[tile % 2] = jnp.broadcast_to(jnp.max(scores, axis=1, keepdims=True), (TILE, width))

    score(0)
    for tile in range(tiles):
        if tile + 1 < tiles:
            score(tile + 1)
        rows = slice(tile * TILE, (tile + 1) * TILE)
        top = tops[tile % 2]
        if not first:
            old = state_in[1][rows, :]
            top = jnp.maximum(old, top)
        weight = jnp.exp2((buffers[tile % 2][...] - top[:, 0:1]) * factor).astype(BF16)
        total = jnp.dot(weight, v_all[...], preferred_element_type=F32)
        if not first:
            shrink = jnp.exp2((old - top) * factor)
            total = total + state_in[0][rows, :] * jnp.concatenate([shrink, shrink], axis=1)
        if not last:
            outs[0][rows, :] = total
            outs[1][rows, :] = top
            continue
        row_sum = total[:, width:]
        mean = (total[:, :width] / row_sum).astype(BF16)
        level = top * scale + jnp.log(row_sum)
        for piece in range(TILE // piece_rows):
            part = slice(piece * piece_rows, (piece + 1) * piece_rows)
            slot = tile * (TILE // piece_rows) + piece
            outs[0][slot, 0:piece_rows, :] = mean[part]
            outs[0][slot, piece_rows : piece_rows + STAT_ROWS, :] = stat_rows(diagonal(level[part]))


def attend(info, entry, gathered, near, far, state, last, scale):
    both, width = near.shape
    count = gathered.shape[0] * 16
    whole = pl.BlockSpec(memory_space=pltpu.VMEM)
    if last:
        shapes = [jax.ShapeDtypeStruct((count // 128, 128 + STAT_ROWS, width), BF16)]
    else:
        shapes = [jax.ShapeDtypeStruct((count, 2 * width), F32), jax.ShapeDtypeStruct((count, width), F32)]
    return pl.pallas_call(
        functools.partial(attend_kernel, scale, not state, last, entry),
        in_specs=[pl.BlockSpec(memory_space=pltpu.SMEM)] + [whole] * (3 + len(state)),
        out_specs=[whole] * len(shapes),
        scratch_shapes=[
            pltpu.VMEM((both, width), BF16),
            pltpu.VMEM((both, 2 * width), BF16),
            pltpu.VMEM((1, both), F32),
            pltpu.VMEM((TILE, both), F32),
            pltpu.VMEM((TILE, both), F32),
            pltpu.VMEM((2, TILE, width), F32),
        ],
        out_shape=shapes,
        name="attend_last" if last else "attend",
        compiler_params=pltpu.CompilerParams(vmem_limit_bytes=20 << 20),
    )(info, gathered, near, far, *state)


def tree_kernel(scale, where_ref, q_ref, tree_ref, parent_ref, accepted_ref, mean_ref, level_ref, picked_ref):
    request, slot = where_ref[0], where_ref[1]
    width = tree_ref.shape[2]
    nodes = parent_ref.shape[0]
    square = (nodes, nodes)
    linked = jnp.logical_or(parent_ref[...] == iota(square, 1), iota(square, 0) == iota(square, 1))
    closure = linked.astype(F32)
    for _ in range(max(nodes - 1, 1).bit_length()):
        narrow = closure.astype(BF16)
        closure = jnp.minimum(jnp.dot(narrow, narrow, preferred_element_type=F32), 1.0)
    queries = q_ref[...].reshape(-1, width)
    count = queries.shape[0]
    heads = q_ref.shape[1]
    of_row = (iota((count, nodes), 0) // heads + slot * (count // heads) == iota((count, nodes), 1)).astype(BF16)
    allowed = jnp.dot(of_row, closure.astype(BF16), preferred_element_type=F32) > 0.5
    tree = tree_ref[...].reshape(-1, width)
    kinds = tree_ref.shape[1]
    column, row = iota((nodes, nodes * kinds), 1), iota((nodes, nodes * kinds), 0)
    pick_k = (column == row * kinds + request).astype(BF16)
    pick_v = (column == row * kinds + request + kinds // 2).astype(BF16)
    keys = jnp.dot(pick_k, tree, preferred_element_type=F32).astype(BF16)
    values = jnp.dot(pick_v, tree, preferred_element_type=F32).astype(BF16)
    scores = lax.dot_general(queries, keys, (((1,), (1,)), ((), ())), preferred_element_type=F32) * scale
    top = jnp.max(jnp.where(allowed, scores, NEG), axis=1, keepdims=True)
    weight = jnp.where(allowed, jnp.exp(scores - top), 0.0)
    row_sum = jnp.sum(weight, axis=1, keepdims=True)
    total = jnp.dot(weight.astype(BF16), values, preferred_element_type=F32)
    mean_ref[...] = total / row_sum
    level = jnp.broadcast_to(top + jnp.log(row_sum), (count, width))
    level_ref[...] = jnp.broadcast_to(diagonal(level), level_ref.shape)
    picks = accepted_ref.shape[0]
    choose = (accepted_ref[...] == iota((picks, nodes * kinds), 1)).astype(BF16)
    picked_ref[...] = jnp.dot(choose, tree, preferred_element_type=F32).astype(BF16)


def tree_part(where, gathered, parent, accepted, scale):
    nodes, rows, width = gathered.shape
    outs = [(128, width), (8, width), (accepted.shape[0], width)]
    return pl.pallas_call(
        functools.partial(tree_kernel, scale),
        grid_spec=pltpu.PrefetchScalarGridSpec(
            num_scalar_prefetch=1,
            grid=(1,),
            in_specs=[
                pl.BlockSpec((8, 16, width), lambda i, w: (w[1], 0, 0)),
                pl.BlockSpec((nodes, 8, width), lambda i, w: (0, rows // 8 - 1, 0)),
                pl.BlockSpec(parent.shape, lambda i, w: (0, 0)),
                pl.BlockSpec(accepted.shape, lambda i, w: (0, 0)),
            ],
            out_specs=[pl.BlockSpec(shape, lambda i, w: (0, 0)) for shape in outs],
        ),
        out_shape=[
            jax.ShapeDtypeStruct(outs[0], F32),
            jax.ShapeDtypeStruct(outs[1], F32),
            jax.ShapeDtypeStruct(outs[2], BF16),
        ],
        name="tree_part",
        compiler_params=pltpu.CompilerParams(vmem_limit_bytes=6 << 20),
    )(where, gathered, gathered, parent, accepted)


def as_columns(lines):
    count, width = lines.shape
    return jnp.transpose(jnp.concatenate([lines, jnp.zeros((width - count, width), F32)], axis=0))


def merge_kernel(parts_ref, mean_ref, level_ref, out_ref):
    sources, _, _ = parts_ref.shape
    rows = mean_ref.shape[0]
    stats = parts_ref[:, rows : rows + STAT_ROWS, :].astype(F32)
    lines = stats[:, 0, :] + stats[:, 1, :] + stats[:, 2, :]
    tree_line = level_ref[0:1, :]
    top = jnp.maximum(jnp.max(lines, axis=0, keepdims=True), tree_line)
    scales, tree_scale = jnp.exp(lines - top), jnp.exp(tree_line - top)
    row_sum = jnp.sum(scales, axis=0, keepdims=True) + tree_scale
    columns = as_columns(jnp.concatenate([scales / row_sum, tree_scale / row_sum], axis=0))
    total = mean_ref[...] * columns[:, sources : sources + 1]
    for source in range(sources):
        total = total + parts_ref[source, 0:rows, :].astype(F32) * columns[:, source : source + 1]
    merged = total.astype(BF16)
    heads, nodes = 16, rows // 16
    square = (rows, rows)
    wanted = (iota(square, 0) % nodes) * heads + iota(square, 0) // nodes
    order = (wanted == iota(square, 1)).astype(BF16)
    ordered = jnp.dot(order, merged, preferred_element_type=F32)
    line = jnp.concatenate([ordered[h * nodes : (h + 1) * nodes, :] for h in range(heads)], axis=1).astype(BF16)
    for target in range(out_ref.shape[0]):
        out_ref[target] = line


def merge(parts, mean, level):
    sources, _, width = parts.shape
    rows = mean.shape[0]
    return pl.pallas_call(
        merge_kernel,
        out_shape=jax.ShapeDtypeStruct((sources, rows // 16, 16 * width), BF16),
        name="merge",
        compiler_params=pltpu.CompilerParams(vmem_limit_bytes=6 << 20),
    )(parts, mean, level)


def project_kernel(core_ref, weight_ref, other_ref, *refs):
    core, parts, out_ref = core_ref[0], refs[:-1], refs[-1]
    half, rows = other_ref.shape[0], parts[0].shape[0]
    features = jnp.concatenate([part[...] for part in parts], axis=0)
    own = weight_ref[pl.ds(pl.multiple_of(core * half, half), half), :]
    for slot, columns in ((core, own), (1 - core, other_ref[...])):
        total = jnp.dot(features, columns, preferred_element_type=F32).astype(BF16)
        for index in range(len(parts)):
            out_ref[index, slot] = total[index * rows : (index + 1) * rows, :]


def project(core, weight, other, *parts):
    rows, columns = parts[0].shape[0], weight.shape[1]
    return pl.pallas_call(
        project_kernel,
        in_specs=[pl.BlockSpec(memory_space=pltpu.SMEM)]
        + [pl.BlockSpec(memory_space=pltpu.VMEM)] * (2 + len(parts)),
        out_shape=jax.ShapeDtypeStruct((len(parts), 2, rows, columns), BF16),
        name="project",
        compiler_params=pltpu.CompilerParams(vmem_limit_bytes=12 << 20),
    )(core, weight, other, *parts)


def append_kernel(info_ref, rows_k, rows_v, keys_in, values_in, keys_out, values_out, sem_k, sem_v):
    local = keys_out.shape[1]
    requests, most = info_ref.shape[0], rows_k.shape[0] // keys_out.shape[0]
    for request in range(requests):
        start, count = info_ref[request, 0], info_ref[request, 1]

        def place(j, carry, request=request, start=start, count=count):
            target = start + j

            @pl.when(jnp.logical_and(j < count, jnp.logical_and(target >= 0, target < local)))
            def _():
                copy_k = pltpu.make_async_copy(rows_k.at[request * most + j], keys_out.at[request, target], sem_k)
                copy_v = pltpu.make_async_copy(rows_v.at[request * most + j], values_out.at[request, target], sem_v)
                copy_k.start()
                copy_v.start()
                copy_k.wait()
                copy_v.wait()

            return carry

        lax.fori_loop(0, most, place, 0)


def append(info, rows_k, rows_v, keys, values):
    anywhere = pl.BlockSpec(memory_space=pl.ANY)
    return pl.pallas_call(
        append_kernel,
        in_specs=[pl.BlockSpec(memory_space=pltpu.SMEM)]
        + [pl.BlockSpec(memory_space=pltpu.VMEM)] * 2
        + [anywhere] * 2,
        out_specs=[anywhere] * 2,
        out_shape=[jax.ShapeDtypeStruct(keys.shape, BF16)] * 2,
        input_output_aliases={3: 0, 4: 1},
        scratch_shapes=[pltpu.SemaphoreType.DMA, pltpu.SemaphoreType.DMA],
        name="append",
        compiler_params=pltpu.CompilerParams(vmem_limit_bytes=2 << 20),
    )(info, rows_k, rows_v, keys, values)


def swap(block):
    return lax.ppermute(block, "c", [(0, 1), (1, 0)])


def passed(block, distance, flip):
    rows = lax.axis_size("x")
    route = [(2 * i + c, 2 * ((i + distance) % rows) + (c + flip) % 2) for i in range(rows) for c in range(2)]
    return lax.ppermute(block, ("x", "c"), route)


def exchange(block, axis):
    return lax.all_to_all(block, axis, 0, 0, tiled=True)


def verify(queries, tree_k, tree_v, cache_k, cache_v, weight, lengths, parents, accepted, accepted_count):
    requests, local, _, width = cache_k.shape
    rows_x, rows_z = lax.axis_size("x"), lax.axis_size("z")
    scale = 1.0 / math.sqrt(width)
    core = lax.axis_index("c")
    x, z = lax.axis_index("x"), lax.axis_index("z")
    index = (x * rows_z + z) * 2 + core
    core_vector = core.astype(jnp.int32)[None]
    low = core == 0
    order = (0, 1, 3, 2)

    here = jnp.stack([x, core]).astype(jnp.int32)
    copy_k, copy_v, *halves = split_heads(here, cache_k.reshape(requests, -1, width), cache_v.reshape(requests, -1, width))
    queries, halves = lax.optimization_barrier((queries, halves))
    packed = pack(
        queries.reshape(requests, -1, width), tree_k.reshape(-1, width), tree_v.reshape(-1, width), rows_z, 2
    )
    blocks = {}
    for distance in order:
        for flip in range(2):
            part = halves[2 * distance + flip]
            blocks[distance, flip] = passed(part, distance, flip) if distance or flip else part
    gathered = exchange(packed.reshape((-1,) + packed.shape[3:]), ("x", "z", "c"))

    half = weight.shape[0] // 2
    given = lax.dynamic_slice_in_dim(weight, (1 - core) * half, half, 0)
    weight_other = swap(given)

    place = jnp.stack([x, z]).astype(jnp.int32)
    parent = lax.dynamic_index_in_dim(parents, x, 0, keepdims=False)[:, None]
    kinds = 2 * requests
    chosen = accepted[None] * kinds + (jnp.arange(kinds, dtype=jnp.int32)).reshape(2, requests, 1)
    tree_mean, tree_level, picked = tree_part(place, gathered, parent, chosen.reshape(-1, 1), scale)

    length = lax.dynamic_index_in_dim(lengths, x, 0, keepdims=False)
    state = ()
    rows = lax.rem(x + rows_x - jnp.arange(rows_x), rows_x)[:, None] * (2 * rows_z) + z * 2
    cores = jnp.stack([core, 1 - core])[None]
    info = (length - (rows + cores) * local).reshape(-1).astype(jnp.int32)
    for distance in order:
        last = distance == order[-1]
        if last:
            state, tree_mean, tree_level, weight_other = lax.optimization_barrier(
                (state, tree_mean, tree_level, weight_other)
            )
        state = attend(info, 2 * distance, gathered, blocks[distance, 0], blocks[distance, 1], state, last, scale)
    near = exchange(state[0], "z")

    spread = exchange(merge(near, tree_mean, tree_level), "z")
    spread = spread.reshape(-1, spread.shape[2])
    moved = {distance: passed(spread, distance, 0) for distance in order[1:]}
    picked, _ = lax.optimization_barrier((picked, spread))
    picked_other = swap(picked)
    both = jnp.stack([jnp.where(low, picked, picked_other), jnp.where(low, picked_other, picked)], axis=1)
    both = both.reshape(2, -1, 2, width)
    target = jnp.stack([lengths - index * local, accepted_count], axis=1).astype(jnp.int32)
    keys_out, values_out = append(
        target, both[0], both[1], copy_k.reshape(cache_k.shape), copy_v.reshape(cache_v.shape)
    )

    shares = [
        project(core_vector, weight, weight_other, spread),
        project(core_vector, weight, weight_other, moved[1], moved[3]),
        project(core_vector, weight, weight_other, moved[2]),
    ]
    shares = jnp.concatenate([shares[0], shares[1][0:1], shares[2], shares[1][1:2]], axis=0)
    turned = jnp.stack([lax.dynamic_index_in_dim(shares, lax.rem(x + rows_x - r, rows_x), 0, False) for r in range(4)])
    shares = exchange(turned.reshape((-1,) + turned.shape[2:]), ("y", "c"))
    projected = jnp.sum(shares.astype(F32), axis=0).astype(BF16)
    return projected, keys_out, values_out


def solution(mesh):
    fine = Mesh(mesh.devices.reshape(4, 8, 2, 4), ("x", "z", "c", "y"))
    seq = ("x", "z", "c")
    cache = P(None, seq, "y", None)
    in_specs = (cache, cache, cache, cache, cache, P("y", seq), P(), P(), P(), P())
    out_specs = (P("y", seq), cache, cache)
    return jax.shard_map(verify, mesh=fine, in_specs=in_specs, out_specs=out_specs, check_vma=False)
```
